256 devices in a mesh: coarse: 8 (over z_hi, x), fine: 8 (over y, core), swath: 4 (over z_lo).
Axes of the slice: x: 4, y: 4, z: 8 (z_hi: 2, z_lo: 4; z = z_hi * 4 + z_lo), core: 2. Of those that a mesh axis runs over, the one named last changes fastest.
Arguments:
- echoes: int32 [256, 64, 2, 2048], P(('coarse', 'fine'), None, None, 'swath'), may hold values from -127 to 127
- exponents: int32 [256, 64, 64], P(('coarse', 'fine'), None, 'swath'), may hold values from 0 to 3
- replica: bfloat16 [2, 129], replicated, may hold values from -0.375 to 0.375
- interp0: bfloat16 [2, 256, 64, 64], P(None, ('coarse', 'fine')), may hold values from -0.5 to 0.5
- upsample1: bfloat16 [2, 256, 64, 512], P(None, ('coarse', 'fine')), may hold values from -0.125 to 0.125
- phase1: bfloat16 [512, 256, 2048], P(None, ('coarse', 'fine'), 'swath'), may hold values from -3.140625 to 3.140625
- upsample2: bfloat16 [16, 2, 512, 2048], P('coarse', None, 'fine'), may hold values from -0.046875 to 0.046875
- phase2: bfloat16 [2048, 16, 2048], P(None, 'coarse', 'swath'), may hold values from -3.140625 to 3.140625
Outputs:
- image: float32 [2048, 2, 2048], P(('coarse', 'fine'), None, 'swath')
The draws below stay inside these ranges and needn't reach their ends.
All inputs are finite; a program needn't handle non-finite values.
Results may differ from the reference program's by a relative error of at most 0.005.
Values may be sent and summed in bfloat16 or wider, within the bound.
No kernel may reach another device: no remote copies, remote signals or barrier semaphores. Data moves between devices by JAX's collectives and lax.ppermute only.
A program may use at most 128 MiB of HBM per device.

```python
import jax
import jax.numpy as jnp
from jax import lax

HALF = 64
QB = 32
L = 64
GROUPS = 2
KIDS = 2
B0 = 64
B1 = 512
B2 = 2048
TAPS = 129
RANGE = 2048
SUBAPS = 256
PARENTS = 16
N_FINE = 8


def with_ends(values, rng, smallest, top_value):
    longest = values.shape.index(max(values.shape))
    spots = []
    for shift in (0, 1):
        where = [jax.random.randint(jax.random.fold_in(rng, axis), (), 0, length) for axis, length in enumerate(values.shape)]
        where[longest] = (where[longest] + shift) % values.shape[longest]
        spots.append(tuple(where))
    return values.at[spots[0]].set(smallest).at[spots[1]].set(top_value)


def steps_of(stream_key, dims, split, low, high):
    def one(dim, blocks):
        steps = jax.random.uniform(jax.random.fold_in(jax.random.fold_in(stream_key, 6), dim), (blocks,), jnp.float32, low / len(split), high / len(split))
        return jnp.repeat(jnp.exp(steps), dims[dim] // blocks).reshape((-1,) + (1,) * (len(dims) - dim - 1))

    loudness = one(*split[0])
    for cut in split[1:]:
        loudness = loudness * one(*cut)
    return loudness


def centred(own_key, dims, scale, limit, split=(), kind=jnp.bfloat16):
    values = scale * jax.random.normal(own_key, dims, jnp.float32)
    if split:
        values = values * steps_of(own_key, dims, split, -0.22, 0.18)
    return jnp.clip(values, -limit, limit).astype(kind)


def setup_inputs(seed: int = 0) -> dict:
    key_list = jax.random.split(jax.random.key(seed), 9)
    echoes = with_ends(jax.random.randint(key_list[0], (SUBAPS, L, 2, RANGE), -127, 128), jax.random.fold_in(key_list[0], 1), -127, 127).astype(jnp.int32)
    exponents = with_ends(jax.random.randint(key_list[1], (SUBAPS, L, RANGE // QB), 0, 4), jax.random.fold_in(key_list[1], 1), 0, 3).astype(jnp.int32)
    replica = centred(key_list[2], (2, TAPS), (2 * TAPS) ** -0.5, 0.375)
    interp0 = centred(key_list[3], (2, SUBAPS, L, B0), (2 * L) ** -0.5, 0.5, ((1, 64),))
    upsample1 = centred(key_list[4], (2, SUBAPS, B0, B1), (2 * B0 * KIDS * N_FINE) ** -0.5, 0.125, ((1, 64),))
    phase1 = jnp.clip(jax.random.uniform(key_list[5], (B1, SUBAPS, RANGE), jnp.float32, -3.140625, 3.140625), -3.140625, 3.140625).astype(jnp.bfloat16)
    upsample2 = centred(key_list[6], (PARENTS, 2, B1, B2), (2 * B1 * PARENTS) ** -0.5, 0.046875, ((0, 8), (2, 8)))
    phase2 = jnp.clip(jax.random.uniform(key_list[7], (B2, PARENTS, RANGE), jnp.float32, -3.140625, 3.140625), -3.140625, 3.140625).astype(jnp.bfloat16)
    return {"echoes": echoes, "exponents": exponents, "replica": replica, "interp0": interp0, "upsample1": upsample1, "phase1": phase1, "upsample2": upsample2, "phase2": phase2}


def level_one(parent, echoes, exponents, kernel, interp0, upsample1, phase1):
    coarse_idx = parent // GROUPS
    group_idx = parent % GROUPS
    fine_ids = jnp.arange(N_FINE).astype(jnp.int32)
    kid_ids = jnp.arange(KIDS).astype(jnp.int32)
    members = ((coarse_idx * N_FINE + fine_ids[:, None]) * (GROUPS * KIDS) + group_idx * KIDS + kid_ids[None, :]).reshape(-1).astype(jnp.int32)
    quant = jnp.take(echoes, members, axis=0)
    expo = jnp.take(exponents, members, axis=0)
    factors = jnp.repeat(jnp.exp2(expo.astype(jnp.float32) - 8.0), QB, axis=2)
    samples = (quant.astype(jnp.float32) * factors[:, :, None, :]).astype(jnp.bfloat16)
    signal = samples.astype(jnp.float32).reshape(-1, 2, RANGE)
    compressed = lax.conv_general_dilated(signal, kernel, (1,), [(HALF, HALF)], precision=lax.Precision.HIGHEST)
    compressed = lax.optimization_barrier(compressed.astype(jnp.bfloat16)).astype(jnp.float32)
    compressed = compressed.reshape(-1, L, 2, RANGE)
    weight_table = jnp.take(interp0, members, axis=1).astype(jnp.float32)
    compressed_real = compressed[:, :, 0]
    compressed_imaginary = compressed[:, :, 1]
    beam_real_part = jnp.einsum("euj,eui->eji", weight_table[0], compressed_real) - jnp.einsum("euj,eui->eji", weight_table[1], compressed_imaginary)
    beam_imaginary_part = jnp.einsum("euj,eui->eji", weight_table[0], compressed_imaginary) + jnp.einsum("euj,eui->eji", weight_table[1], compressed_real)
    beam_real_part = lax.optimization_barrier(beam_real_part.astype(jnp.bfloat16)).astype(jnp.float32)
    beam_imaginary_part = lax.optimization_barrier(beam_imaginary_part.astype(jnp.bfloat16)).astype(jnp.float32)
    upper_bound = jnp.take(upsample1, members, axis=1).astype(jnp.float32)
    upsampled_real = jnp.einsum("xyj,xya->xja", upper_bound[0], beam_real_part) - jnp.einsum("xyj,xya->xja", upper_bound[1], beam_imaginary_part)
    upsampled_imaginary = jnp.einsum("xyj,xya->xja", upper_bound[0], beam_imaginary_part) + jnp.einsum("xyj,xya->xja", upper_bound[1], beam_real_part)
    angles = jnp.transpose(jnp.take(phase1, members, axis=1).astype(jnp.float32), (1, 0, 2))
    cosine = jnp.cos(angles)
    sine = jnp.sin(angles)
    level_re = jnp.sum(cosine * upsampled_real - sine * upsampled_imaginary, axis=0)
    level_im = jnp.sum(sine * upsampled_real + cosine * upsampled_imaginary, axis=0)
    level_re = lax.optimization_barrier(level_re.astype(jnp.bfloat16)).astype(jnp.float32)
    level_im = lax.optimization_barrier(level_im.astype(jnp.bfloat16)).astype(jnp.float32)
    return level_re, level_im


def reference(echoes, exponents, replica, interp0, upsample1, phase1, upsample2, phase2):
    tap_re = replica[0].astype(jnp.float32)
    tap_im = replica[1].astype(jnp.float32)
    kernel = jnp.stack([jnp.stack([tap_re, tap_im]), jnp.stack([-tap_im, tap_re])])

    def step(carry, parent):
        level_re, level_im = level_one(parent, echoes, exponents, kernel, interp0, upsample1, phase1)
        upper_bound = lax.dynamic_index_in_dim(upsample2, parent, 0, keepdims=False).astype(jnp.float32)
        val_re = jnp.dot(upper_bound[0].T, level_re, precision=lax.Precision.HIGHEST) - jnp.dot(upper_bound[1].T, level_im, precision=lax.Precision.HIGHEST)
        val_im = jnp.dot(upper_bound[0].T, level_im, precision=lax.Precision.HIGHEST) + jnp.dot(upper_bound[1].T, level_re, precision=lax.Precision.HIGHEST)
        angles = lax.dynamic_index_in_dim(phase2, parent, 1, keepdims=False).astype(jnp.float32)
        cosine = jnp.cos(angles)
        sine = jnp.sin(angles)
        term = jnp.stack([cosine * val_re - sine * val_im, sine * val_re + cosine * val_im], axis=1)
        return carry + term, None

    start_image = jnp.zeros((B2, 2, RANGE), jnp.float32)
    parents_all = jnp.arange(PARENTS).astype(jnp.int32)
    image, _ = lax.scan(step, start_image, parents_all)
    return image
```

```python
import jax
import jax.numpy as jnp
from jax import lax
from jax.sharding import PartitionSpec as P


def with_halo(shard, sides, width):
    for axis, dim in sides:
        size, length = (lax.axis_size(axis), shard.shape[dim])
        up = [(i, (i + 1) % size) for i in range(size - 1)]
        down = [(j, i) for i, j in up]
        last = lax.slice_in_dim(shard, length - width, length, axis=dim)
        first = lax.slice_in_dim(shard, 0, width, axis=dim)
        before = lax.ppermute(last, axis, up)
        after = lax.ppermute(first, axis, down)
        shard = jnp.concatenate([before, shard, after], axis=dim)
    return shard


def band_matrix(taps, window, out_bins):
    line = jnp.concatenate([taps, jnp.zeros((window + 1 - taps.shape[0],), taps.dtype)])
    flat = jnp.tile(line, out_bins)[: out_bins * window]
    return flat.reshape(out_bins, window).T


def complex_mixer(real_part, imag_part):
    first = jnp.stack([real_part, imag_part], axis=-2)
    second = jnp.stack([-imag_part, real_part], axis=-2)
    return jnp.stack([first, second], axis=1)


def swap_cores(x):
    return lax.ppermute(x, "fine", [(i, i ^ 1) for i in range(8)])


def shift_chips(x, d):
    return lax.ppermute(x, "fine", [(y * 2 + k, (y + d) % 4 * 2 + k) for y in range(4) for k in range(2)])


def shift_x(x, d):
    return lax.ppermute(x, "coarse", [(z * 4 + i, z * 4 + (i + d) % 4) for z in range(2) for i in range(4)])


def swap_z(x):
    return lax.ppermute(x, "coarse", [(i, i ^ 4) for i in range(8)])


def pick(x, i, axis=0):
    return lax.dynamic_index_in_dim(x, i, axis, keepdims=False)


def rotate(re, im, angles):
    radians = angles.astype(jnp.float32)
    cosine = jnp.cos(radians)
    sine = jnp.sin(radians)
    return cosine * re - sine * im, sine * re + cosine * im


def shards(echoes, exponents, replica, interp0, upsample1, phase1, upsample2, phase2):
    fine = lax.axis_index("fine")
    coarse = lax.axis_index("coarse")
    y = fine // 2
    k = fine % 2
    cx = coarse % 4
    cz = coarse // 4
    sub_count, ping_count, _, range_bins = echoes.shape
    half_taps = (replica.shape[1] - 1) // 2
    quant_block = range_bins // exponents.shape[2]
    u2_own = pick(upsample2, k)
    u2_recv = swap_cores(pick(upsample2, 1 - k))
    u2_rows = jnp.where(k == 0, jnp.stack([u2_own, u2_recv]), jnp.stack([u2_recv, u2_own]))
    u2_rows = jnp.transpose(u2_rows.reshape(2, 2, 64, 8, 4, 64), (4, 1, 0, 2, 3, 5)).reshape(4, 2, 128, 512)
    u2_parts = [pick(u2_rows, y)] + [shift_chips(pick(u2_rows, (y + d) % 4), d) for d in (1, 2, 3)]
    u1_group = upsample1.reshape(2, 2, 2, 64, 512)
    u1_all = jnp.concatenate([pick(u1_group, k, 1), swap_cores(pick(u1_group, 1 - k, 1))], axis=1)
    ph_group = jnp.transpose(phase1, (1, 0, 2)).reshape(2, 2, 512, range_bins)
    ph_all = jnp.concatenate([pick(ph_group, k), swap_cores(pick(ph_group, 1 - k))], axis=0)

    factors = jnp.repeat(jnp.exp2(exponents.astype(jnp.float32) - 8.0), quant_block, axis=2)
    samples = (echoes.astype(jnp.float32) * factors[:, :, None, :]).astype(jnp.bfloat16)
    padded = with_halo(samples, (("swath", 3),), half_taps)
    tile_bins = 128
    tile_count = range_bins // tile_bins
    window = tile_bins + 2 * half_taps
    real_band = band_matrix(replica[0], window, tile_bins)
    imag_band = band_matrix(replica[1], window, tile_bins)
    kernel = jnp.concatenate(
        [
            jnp.concatenate([real_band, -imag_band], axis=1),
            jnp.concatenate([imag_band, real_band], axis=1),
        ],
        axis=0,
    )
    pieces = []
    for tile in range(tile_count):
        segment = padded[:, :, :, tile * tile_bins : tile * tile_bins + window]
        product = jnp.dot(
            segment.reshape(sub_count * ping_count, 2 * window),
            kernel,
            preferred_element_type=jnp.float32,
        )
        pieces.append(product.astype(jnp.bfloat16).reshape(sub_count, ping_count, 2, tile_bins))
    compressed = jnp.concatenate(pieces, axis=3)
    mixer_zero = complex_mixer(interp0[0], interp0[1])
    beams = jnp.einsum(
        "silob,slir->sobr", mixer_zero, compressed, preferred_element_type=jnp.float32
    ).astype(jnp.bfloat16)
    beam_group = beams.reshape(2, 2, 2, 64, range_bins)
    beams_all = jnp.concatenate([pick(beam_group, k), swap_cores(pick(beam_group, 1 - k))], axis=0)

    mixer = complex_mixer(u1_all[0], u1_all[1])
    turned = jnp.einsum("sibon,sibr->sonr", mixer, beams_all, preferred_element_type=jnp.float32)
    re, im = rotate(turned[:, 0], turned[:, 1], ph_all)
    part = jnp.stack([jnp.sum(re, axis=0), jnp.sum(im, axis=0)]).astype(jnp.bfloat16)
    part = jnp.transpose(part.reshape(2, 4, 128, range_bins), (1, 0, 2, 3))
    total = pick(part, y).astype(jnp.float32)
    for d in (1, 2, 3):
        total += shift_chips(pick(part, (y + d) % 4), d).astype(jnp.float32)
    level = total.astype(jnp.bfloat16)
    levels = [level] + [shift_chips(level, d) for d in (1, 2, 3)]
    out_re = 0.0
    out_im = 0.0
    for u, v in zip(u2_parts, levels):
        dot = lambda a, b: jnp.einsum("nm,nr->mr", a, b, preferred_element_type=jnp.float32)
        out_re += dot(u[0], v[0]) - dot(u[1], v[1])
        out_im += dot(u[0], v[1]) + dot(u[1], v[0])
    ph2 = pick(pick(phase2.reshape(8, 4, 64, 2, range_bins), y, 1), k, 2).reshape(512, range_bins)
    re, im = rotate(out_re, out_im, ph2)
    image = jnp.stack([re, im], axis=1).reshape(8, 2, 32, 2, range_bins)
    total = pick(image, k, 1) + swap_cores(pick(image, 1 - k, 1).astype(jnp.bfloat16)).astype(jnp.float32)
    total = total.reshape(2, 4, 32, 2, range_bins)
    narrow = total.astype(jnp.bfloat16)
    share = pick(total, cx, 1)
    for d in (1, 2, 3):
        share += shift_x(pick(narrow, (cx + d) % 4, 1), d).astype(jnp.float32)
    return pick(share, cz) + swap_z(pick(share, 1 - cz).astype(jnp.bfloat16)).astype(jnp.float32)


def solution(mesh):
    in_specs = (
        P(("coarse", "fine"), None, None, "swath"),
        P(("coarse", "fine"), None, "swath"),
        P(),
        P(None, ("coarse", "fine"), None, None),
        P(None, ("coarse", "fine"), None, None),
        P(None, ("coarse", "fine"), "swath"),
        P("coarse", None, "fine", None),
        P(None, "coarse", "swath"),
    )
    out_specs = P(("coarse", "fine"), None, "swath")
    return jax.shard_map(shards, mesh=mesh, in_specs=in_specs, out_specs=out_specs, check_vma=False)
```

```python
import jax
import jax.numpy as jnp
from jax import lax
from jax.experimental import pallas as pl
from jax.experimental.pallas import tpu as pltpu
from jax.sharding import PartitionSpec as P

F32 = jnp.float32
BF16 = jnp.bfloat16

SIN = (0.7071067690849304, -0.029462749138474464, 0.0003682656097225845, -2.1877108338230755e-06, 7.155278591852721e-09)
COS = (1.4142135381698608, -0.17677636444568634, 0.003682575421407819, -3.061265670112334e-05, 1.279087769034959e-07)
VMEM = pltpu.MemorySpace.VMEM
PARAMS = pltpu.CompilerParams(vmem_limit_bytes=16 << 20)
WHOLE = pl.BlockSpec(memory_space=pltpu.MemorySpace.VMEM)


def horner(u, coefs):
    total = coefs[-1] * u + coefs[-2]
    for c in coefs[-3::-1]:
        total = total * u + c
    return total


def cos_sin(x):
    u = x * x
    s = x * horner(u, SIN)
    return 1.0 - s * s, s * horner(u, COS)


def near(x):
    return pltpu.with_memory_space_constraint(x, VMEM)


def swap_cores(x):
    return lax.ppermute(x, "fine", [(i, i ^ 1) for i in range(8)])


def shift_chips(x, d):
    return lax.ppermute(x, "fine", [(y * 2 + k, (y + d) % 4 * 2 + k) for y in range(4) for k in range(2)])


def shift_x(x, d):
    return lax.ppermute(x, "coarse", [(z * 4 + i, z * 4 + (i + d) % 4) for z in range(2) for i in range(4)])


def swap_z(x):
    return lax.ppermute(x, "coarse", [(i, i ^ 4) for i in range(8)])


def pick(x, i, axis=0):
    return lax.dynamic_index_in_dim(x, i, axis, keepdims=False)


def tdot(a, b):
    return lax.dot_general(a, b, (((0,), (0,)), ((), ())), preferred_element_type=F32)


def factors(expo, lo, lanes):
    blocks = expo.shape[0]
    bins = lo + lax.broadcasted_iota(jnp.int32, (blocks, lanes), 1)
    expand = bins // 32 == lax.broadcasted_iota(jnp.int32, (blocks, lanes), 0)
    scale = (jnp.left_shift(1, expo).astype(F32) * (1.0 / 256.0)).astype(BF16)
    return tdot(scale, expand.astype(F32).astype(BF16))


def ends_kernel(low_ref, high_ref, expo_ref, first_ref, last_ref):
    subs, pings, _, lanes = low_ref.shape
    low = lax.broadcasted_iota(jnp.int32, (pings, lanes), 1) < 64
    start = 32 * expo_ref.shape[1] - lanes
    for s in range(subs):
        factor = factors(expo_ref[s], 0, lanes)
        re = low_ref[s, :, 0, :].astype(F32) * factor
        im = low_ref[s, :, 1, :].astype(F32) * factor
        first_ref[s] = jnp.where(low, re, pltpu.roll(im, 64, 1)).astype(BF16)
        factor = factors(expo_ref[s], start, lanes)
        re = high_ref[s, :, 0, :].astype(F32) * factor
        im = high_ref[s, :, 1, :].astype(F32) * factor
        last_ref[s] = jnp.where(low, pltpu.roll(re, 64, 1), im).astype(BF16)


def ends(echoes, exponents):
    s, l, _, r = echoes.shape
    b = exponents.shape[1]
    shape = jax.ShapeDtypeStruct((s, l, 128), BF16)
    whole = pl.BlockSpec((s, l, 128), lambda i: (0, 0, 0))
    return pl.pallas_call(
        ends_kernel,
        grid=(1,),
        in_specs=[
            pl.BlockSpec((s, l, 2, 128), lambda i: (0, 0, 0, 0)),
            pl.BlockSpec((s, l, 2, 128), lambda i: (0, 0, 0, r // 128 - 1)),
            pl.BlockSpec((s, b, l), lambda i: (0, 0, 0)),
        ],
        out_specs=[whole, whole],
        out_shape=[shape, shape],
        name="ends",
        compiler_params=PARAMS,
    )(echoes, echoes, exponents)


def prep_kernel(echo_ref, expo_ref, out_ref):
    for s in range(echo_ref.shape[0]):
        factor = factors(expo_ref[s], 0, echo_ref.shape[3])
        for i in (0, 1):
            out_ref[s, i] = (echo_ref[s, :, i, :].astype(F32) * factor).astype(BF16)


def prep(echoes, exponents):
    s, l, _, r = echoes.shape
    b = exponents.shape[1]
    return pl.pallas_call(
        prep_kernel,
        grid=(2,),
        in_specs=[
            pl.BlockSpec((s // 2, l, 2, r), lambda i: (i, 0, 0, 0)),
            pl.BlockSpec((s // 2, b, l), lambda i: (i, 0, 0)),
        ],
        out_specs=pl.BlockSpec((s // 2, 2, l, r), lambda i: (i, 0, 0, 0)),
        out_shape=jax.ShapeDtypeStruct((s, 2, l, r), BF16),
        name="prep",
        compiler_params=PARAMS,
    )(echoes, exponents)


def core():
    return lax.axis_index("fine") & 1


def pack_kernel(own_ref, other_ref, *out_refs):
    fine = lax.axis_index("fine")
    k = fine & 1
    rows = own_ref.shape[2]
    low = lax.broadcasted_iota(jnp.int32, (rows, 128), 1) < 64
    for d, out in enumerate(out_refs):
        y = ((fine >> 1) + d) & 3
        even = (y & 1) == 0
        base = pl.multiple_of((y >> 1) * 128, 128)
        for ref, half in ((own_ref, k), (other_ref, 1 - k)):
            at = pl.ds(pl.multiple_of(half * rows, rows), rows)
            for i in (0, 1):
                for p in range(4):
                    a = ref[0, i, :, pl.ds(base + p * 512, 128)].astype(F32)
                    b = ref[0, i, :, pl.ds(base + p * 512 + 256, 128)].astype(F32)
                    c = jnp.where(even, b, a)
                    c = pltpu.roll(c, 64, 1)
                    out[i, at, p * 128 : (p + 1) * 128] = jnp.where(low, jnp.where(even, a, c), jnp.where(even, c, b)).astype(BF16)


def pack(own, other):
    _, i, rows, m = own.shape
    shape = jax.ShapeDtypeStruct((2, 2 * rows, m // 4), BF16)
    window = pl.BlockSpec((1, i, rows, m), lambda g: (core(), 0, 0, 0))
    return pl.pallas_call(
        pack_kernel,
        grid=(1,),
        in_specs=[window, window],
        out_specs=[pl.BlockSpec(shape.shape, lambda g: (0, 0, 0))] * 4,
        out_shape=[shape] * 4,
        name="pack",
        compiler_params=PARAMS,
    )(own, other)


def weights_kernel(u_own, u_other, ph_other, mix_ref, ph_ref):
    kids = u_own.shape[1]
    for i, u in enumerate((u_own, u_other)):
        for s in range(kids):
            ur = u[0, s]
            ui = u[1, s]
            mix_ref[i * kids + s, 0] = jnp.concatenate([ur, -ui], axis=0).T
            mix_ref[i * kids + s, 1] = jnp.concatenate([ui, ur], axis=0).T
    ph_ref[...] = ph_other[...]


def weights(u_own, u_other, ph_other):
    i, s, b, n = u_own.shape
    _, _, r = ph_other.shape
    kids = s // 2
    window = pl.BlockSpec((i, kids, b, n), lambda g: (0, core(), 0, 0))
    return pl.pallas_call(
        weights_kernel,
        grid=(1,),
        in_specs=[window, window, pl.BlockSpec((kids, n, r), lambda g: (core(), 0, 0))],
        out_specs=[WHOLE, WHOLE],
        out_shape=[pltpu.VMEM((s, 2, n, 2 * b), BF16), pltpu.VMEM((kids, n, r), BF16)],
        name="weights",
        compiler_params=PARAMS,
    )(u_own, u_other, ph_other)


def band_kernel(line_ref, band_ref):
    def band(row):
        full = jnp.broadcast_to(line_ref[row : row + 1, :], (384, 512))
        return pltpu.roll(full, 448, 1, stride=1, stride_axis=0)[:, :128]

    hr = band(0)
    hi = band(1)
    band_ref[0] = jnp.concatenate([hr, -hi], axis=1).astype(BF16)
    band_ref[1] = jnp.concatenate([hi, hr], axis=1).astype(BF16)


def bands(replica):
    taps = replica.astype(F32)
    line = jnp.concatenate([taps[:, :1], jnp.zeros((2, 383), F32), taps[:, :0:-1]], axis=1)
    return pl.pallas_call(band_kernel, out_shape=jax.ShapeDtypeStruct((2, 384, 256), BF16), name="bands", compiler_params=PARAMS)(line)


def beams_kernel(x_ref, left_ref, right_ref, band_ref, w_ref, out_ref):
    subs, _, pings, bins = x_ref.shape
    rows = subs * pings
    tiles = bins // 128

    def tile(ri, j):
        return x_ref[:, ri, :, j * 128 : (j + 1) * 128].reshape(rows, 128)

    cre = []
    cim = []
    for j in range(tiles):
        near = [t for t in (j - 1, j, j + 1) if 0 <= t < tiles]
        lhs = [tile(ri, t) for ri in (0, 1) for t in near]
        lo = 128 * (near[0] - j + 1)
        hi = 128 * (near[-1] - j + 2)
        rhs = [band_ref[0, lo:hi], band_ref[1, lo:hi]]
        if j == 0:
            lhs.append(left_ref[...].reshape(rows, 128))
            rhs += [band_ref[0, 64:128], band_ref[1, 64:128]]
        if j == tiles - 1:
            lhs.append(right_ref[...].reshape(rows, 128))
            rhs += [band_ref[0, 256:320], band_ref[1, 256:320]]
        c = jnp.dot(jnp.concatenate(lhs, axis=1), jnp.concatenate(rhs, axis=0), preferred_element_type=F32)
        cre.append(c[:, :128].astype(BF16))
        cim.append(c[:, 128:].astype(BF16))
    for s in range(subs):
        part = slice(s * pings, (s + 1) * pings)
        c = jnp.concatenate([jnp.concatenate([t[part] for t in cre], axis=1), jnp.concatenate([t[part] for t in cim], axis=1)], axis=0)
        wr = w_ref[0, s]
        wi = w_ref[1, s]
        out_ref[s, 0] = tdot(jnp.concatenate([wr, -wi], axis=0), c).astype(BF16)
        out_ref[s, 1] = tdot(jnp.concatenate([wi, wr], axis=0), c).astype(BF16)


def beams_of(samples, left, right, band, interp0):
    s, _, l, r = samples.shape
    b = interp0.shape[3]
    return pl.pallas_call(beams_kernel, out_shape=pltpu.VMEM((s, 2, b, r), BF16), name="beams", compiler_params=PARAMS)(
        samples, left, right, band, interp0
    )


def level_kernel(d, mix_ref, ph_own, ph_other, b_own, b_other, out_ref, turn_ref):
    fine = lax.axis_index("fine")
    k = fine & 1
    kids = ph_other.shape[0]
    n = out_ref.shape[1]
    base = pl.multiple_of((((fine >> 1) + d) & 3) * n, n)
    rows = pl.ds(base, n)
    for i, b in enumerate((b_own, b_other)):
        for s in range(kids):
            rhs = b[k * kids + s].reshape(-1, b.shape[3])
            for c in (0, 1):
                turn_ref[i * kids + s, c] = jnp.dot(mix_ref[i * kids + s, c, rows, :], rhs, preferred_element_type=F32)

    step = 16

    def body(j, carry):
        at = pl.ds(pl.multiple_of(j * step, step), step)
        there = pl.ds(pl.multiple_of(base + j * step, step), step)
        re = im = None
        for i, (ph, first) in enumerate(((ph_own, k * kids), (ph_other, 0))):
            for s in range(kids):
                c, t = cos_sin(ph[first + s, there, :].astype(F32))
                tr = turn_ref[i * kids + s, 0, at, :]
                ti = turn_ref[i * kids + s, 1, at, :]
                pr = c * tr - t * ti
                pi = t * tr + c * ti
                re = pr if re is None else re + pr
                im = pi if im is None else im + pi
        out_ref[0, at, :] = re.astype(out_ref.dtype)
        out_ref[1, at, :] = im.astype(out_ref.dtype)
        return carry

    lax.fori_loop(0, n // step, body, 0)


def level_part(d, dtype, *operands):
    mix, ph = operands[:2]
    s, _, n, _ = mix.shape
    n //= 4
    r = ph.shape[2]
    return pl.pallas_call(
        lambda *refs: level_kernel(d, *refs),
        in_specs=[WHOLE] * 5,
        out_specs=WHOLE,
        scratch_shapes=[pltpu.VMEM((s, 2, n, r), F32)],
        out_shape=pltpu.VMEM((2, n, r), dtype),
        name="level",
        compiler_params=PARAMS,
    )(*[near(x) for x in operands])


def turn_kernel(ph_ref, out_ref):
    step = 16

    def body(j, carry):
        at = pl.ds(pl.multiple_of(j * step, step), step)
        c, s = cos_sin(ph_ref[at, :].astype(F32))
        out_ref[0, at, :] = c
        out_ref[1, at, :] = s
        return carry

    lax.fori_loop(0, ph_ref.shape[0] // step, body, 0)


def turns(ph):
    return pl.pallas_call(
        turn_kernel,
        in_specs=[WHOLE],
        out_specs=WHOLE,
        out_shape=pltpu.VMEM((2,) + ph.shape, F32),
        name="turns",
        compiler_params=PARAMS,
    )(near(ph))


def image_kernel(*refs):
    us = refs[0:4]
    vs = refs[4:8]
    turn_ref, keep_ref, send_ref, acc_ref = refs[8:]
    own = core() == 0
    rhs = jnp.concatenate([v[i] for v in vs for i in (0, 1)], axis=0)
    acc_ref[0] = tdot(jnp.concatenate([x for u in us for x in (u[0], -u[1])], axis=0), rhs)
    acc_ref[1] = tdot(jnp.concatenate([x for u in us for x in (u[1], u[0])], axis=0), rhs)

    def body(c, carry):
        x = c & 3
        z = c >> 2
        halves = []
        for h in (0, 1):
            at = pl.ds(pl.multiple_of(c * 64 + h * 32, 32), 32)
            co = turn_ref[0, at, :]
            si = turn_ref[1, at, :]
            re = acc_ref[0, at, :]
            im = acc_ref[1, at, :]
            halves.append((co * re - si * im, si * re + co * im))
        for i in (0, 1):
            keep_ref[x, z, i] = jnp.where(own, halves[0][i], halves[1][i])
            send_ref[x, z, i] = jnp.where(own, halves[1][i], halves[0][i]).astype(BF16)
        return carry

    lax.fori_loop(0, 8, body, 0)


def image_parts(us, vs, turn):
    _, m, r = turn.shape
    shape = (4, 2, 2, m // 16, r)
    return pl.pallas_call(
        image_kernel,
        in_specs=[WHOLE] * 9,
        out_specs=[WHOLE, WHOLE],
        scratch_shapes=[pltpu.VMEM((2, m, r), F32)],
        out_shape=[pltpu.VMEM(shape, F32), pltpu.VMEM(shape, BF16)],
        name="image",
        compiler_params=PARAMS,
    )(*[near(x) for x in us], *[near(x) for x in vs], near(turn))


def finish_kernel(near_ref, far_ref, out_ref):
    for i in (0, 1):
        out_ref[:, i, :] = near_ref[i] + far_ref[i].astype(F32)


def finish(share, far):
    i, m, r = share.shape
    return pl.pallas_call(
        finish_kernel,
        in_specs=[WHOLE, WHOLE],
        out_specs=WHOLE,
        out_shape=jax.ShapeDtypeStruct((m, i, r), F32),
        name="finish",
        compiler_params=PARAMS,
    )(near(share), near(far))


def shards(echoes, exponents, replica, interp0, upsample1, phase1, upsample2, phase2):
    fine = lax.axis_index("fine")
    coarse = lax.axis_index("coarse")
    y = fine // 2
    k = fine % 2
    cx = coarse % 4
    cz = coarse // 4
    range_bins = echoes.shape[3]

    expo = jnp.transpose(exponents, (0, 2, 1))
    first, last = ends(echoes, expo)
    size = lax.axis_size("swath")
    left = lax.ppermute(last, "swath", [(i, i + 1) for i in range(size - 1)])
    right = lax.ppermute(first, "swath", [(i + 1, i) for i in range(size - 1)])
    u2_other = swap_cores(upsample2)
    u1_other = swap_cores(upsample1)
    ph_own = jnp.transpose(phase1, (1, 0, 2))
    ph_other = swap_cores(ph_own)
    band = bands(replica)
    u2_parts = pack(upsample2, u2_other)
    samples = prep(echoes, expo)
    u2_parts = [u2_parts[0]] + [shift_chips(u2_parts[d], d) for d in (1, 2, 3)]

    b_own = beams_of(samples, left, right, band, interp0)
    b_other = swap_cores(b_own)

    mix, ph_other = weights(upsample1, u1_other, ph_other)
    operands = (mix, ph_own, ph_other, b_own, b_other)
    received = [shift_chips(level_part(d, BF16, *operands), d) for d in (2, 1, 3)]
    total = level_part(0, F32, *operands)
    for part in received:
        total += part.astype(F32)
    level = total.astype(BF16)
    levels = [level] + [shift_chips(level, d) for d in (1, 2, 3)]

    ph2 = pick(pick(phase2.reshape(8, 4, 64, 2, range_bins), y, 1), k, 2).reshape(512, range_bins)
    turn = turns(ph2)

    keep, send = image_parts(u2_parts, levels, turn)
    other = swap_cores(send)
    narrow = (keep + other.astype(F32)).astype(BF16)
    share = pick(keep, cx) + pick(other, cx).astype(F32)
    for d in (2, 1, 3):
        share += shift_x(pick(narrow, (cx + d) % 4), d).astype(F32)
    return finish(pick(share, cz), swap_z(pick(share, 1 - cz).astype(BF16)))


def solution(mesh):
    in_specs = (
        P(("coarse", "fine"), None, None, "swath"),
        P(("coarse", "fine"), None, "swath"),
        P(),
        P(None, ("coarse", "fine"), None, None),
        P(None, ("coarse", "fine"), None, None),
        P(None, ("coarse", "fine"), "swath"),
        P("coarse", None, "fine", None),
        P(None, "coarse", "swath"),
    )
    out_specs = P(("coarse", "fine"), None, "swath")
    return jax.shard_map(shards, mesh=mesh, in_specs=in_specs, out_specs=out_specs, check_vma=False)
```

```python
import jax
import jax.numpy as jnp
from jax import lax
from jax.experimental import pallas as pl
from jax.experimental.pallas import tpu as pltpu
from jax.sharding import PartitionSpec as P


F32 = jnp.float32
BF16 = jnp.bfloat16

SIN = (0.7071067690849304, -0.029462749138474464, 0.0003682656097225845, -2.1877108338230755e-06, 7.155278591852721e-09)
COS = (1.4142135381698608, -0.17677636444568634, 0.003682575421407819, -3.061265670112334e-05, 1.279087769034959e-07)
VMEM = pltpu.MemorySpace.VMEM
PARAMS = pltpu.CompilerParams(vmem_limit_bytes=16 << 20)
WHOLE = pl.BlockSpec(memory_space=pltpu.MemorySpace.VMEM)


def horner(u, coefs):
    total = coefs[-1] * u + coefs[-2]
    for c in coefs[-3::-1]:
        total = total * u + c
    return total


def cos_sin(x):
    u = x * x
    s = x * horner(u, SIN)
    return 1.0 - s * s, s * horner(u, COS)


def near(x):
    return pltpu.with_memory_space_constraint(x, VMEM)


def swap_cores(x):
    return lax.ppermute(x, "fine", [(i, i ^ 1) for i in range(8)])


def shift_chips(x, d):
    return lax.ppermute(x, "fine", [(y * 2 + k, (y + d) % 4 * 2 + k) for y in range(4) for k in range(2)])


def shift_x(x, d):
    return lax.ppermute(x, "coarse", [(z * 4 + i, z * 4 + (i + d) % 4) for z in range(2) for i in range(4)])


def swap_z(x):
    return lax.ppermute(x, "coarse", [(i, i ^ 4) for i in range(8)])


def pick(x, i, axis=0):
    return lax.dynamic_index_in_dim(x, i, axis, keepdims=False)


def tdot(a, b):
    return lax.dot_general(a, b, (((0,), (0,)), ((), ())), preferred_element_type=F32)


def factors(expo, lo, lanes):
    blocks = expo.shape[0]
    bins = lo + lax.broadcasted_iota(jnp.int32, (blocks, lanes), 1)
    expand = bins // 32 == lax.broadcasted_iota(jnp.int32, (blocks, lanes), 0)
    scale = (jnp.left_shift(1, expo).astype(F32) * (1.0 / 256.0)).astype(BF16)
    return tdot(scale, expand.astype(F32).astype(BF16))


def ends_kernel(low_ref, high_ref, expo_ref, even_ref, odd_ref):
    odd = (lax.axis_index("swath") & 1) == 1
    subs, pings, _, lanes = low_ref.shape
    low = lax.broadcasted_iota(jnp.int32, (pings, lanes), 1) < 64
    start = 32 * expo_ref.shape[1] - lanes
    for s in range(subs):
        factor = factors(expo_ref[s], 0, lanes)
        re = low_ref[s, :, 0, :].astype(F32) * factor
        im = low_ref[s, :, 1, :].astype(F32) * factor
        first = jnp.where(low, re, pltpu.roll(im, 64, 1))
        factor = factors(expo_ref[s], start, lanes)
        re = high_ref[s, :, 0, :].astype(F32) * factor
        im = high_ref[s, :, 1, :].astype(F32) * factor
        last = jnp.where(low, pltpu.roll(re, 64, 1), im)
        even_ref[s] = jnp.where(odd, first, last).astype(BF16)
        odd_ref[s] = jnp.where(odd, last, first).astype(BF16)


def ends(echoes, exponents):
    s, l, _, r = echoes.shape
    b = exponents.shape[1]
    shape = jax.ShapeDtypeStruct((s, l, 128), BF16)
    whole = pl.BlockSpec((s, l, 128), lambda i: (0, 0, 0))
    return pl.pallas_call(
        ends_kernel,
        grid=(1,),
        in_specs=[
            pl.BlockSpec((s, l, 2, 128), lambda i: (0, 0, 0, 0)),
            pl.BlockSpec((s, l, 2, 128), lambda i: (0, 0, 0, r // 128 - 1)),
            pl.BlockSpec((s, b, l), lambda i: (0, 0, 0)),
        ],
        out_specs=[whole, whole],
        out_shape=[shape, shape],
        name="ends",
        compiler_params=PARAMS,
    )(echoes, echoes, exponents)


def prep_kernel(echo_ref, expo_ref, out_ref):
    for s in range(echo_ref.shape[0]):
        factor = factors(expo_ref[s], 0, echo_ref.shape[3])
        for i in (0, 1):
            out_ref[s, i] = (echo_ref[s, :, i, :].astype(F32) * factor).astype(BF16)


def prep(echoes, exponents):
    s, l, _, r = echoes.shape
    b = exponents.shape[1]
    return pl.pallas_call(
        prep_kernel,
        grid=(2,),
        in_specs=[
            pl.BlockSpec((s // 2, l, 2, r), lambda i: (i, 0, 0, 0)),
            pl.BlockSpec((s // 2, b, l), lambda i: (i, 0, 0)),
        ],
        out_specs=pl.BlockSpec((s // 2, 2, l, r), lambda i: (i, 0, 0, 0)),
        out_shape=jax.ShapeDtypeStruct((s, 2, l, r), BF16),
        name="prep",
        compiler_params=PARAMS,
    )(echoes, exponents)


def core():
    return lax.axis_index("fine") & 1


def pack_kernel(own_ref, other_ref, *out_refs):
    fine = lax.axis_index("fine")
    k = fine & 1
    rows = own_ref.shape[2]
    low = lax.broadcasted_iota(jnp.int32, (rows, 128), 1) < 64
    for d, out in enumerate(out_refs):
        y = ((fine >> 1) + d) & 3
        even = (y & 1) == 0
        base = pl.multiple_of((y >> 1) * 128, 128)
        for ref, half in ((own_ref, k), (other_ref, 1 - k)):
            at = pl.ds(pl.multiple_of(half * rows, rows), rows)
            for p in range(4):
                a = ref[0, 0, :, pl.ds(base + p * 512, 128)].astype(F32)
                b = ref[0, 0, :, pl.ds(base + p * 512 + 256, 128)].astype(F32)
                c = pltpu.roll(jnp.where(even, b, a), 64, 1)
                out[0, at, p * 128 : (p + 1) * 128] = jnp.where(low, jnp.where(even, a, c), jnp.where(even, c, b)).astype(BF16)


def pack(own, other):
    _, i, rows, m = own.shape
    shape = jax.ShapeDtypeStruct((2, 2 * rows, m // 4), BF16)
    window = pl.BlockSpec((1, 1, rows, m), lambda g: (core(), g, 0, 0))
    return pl.pallas_call(
        pack_kernel,
        grid=(i,),
        in_specs=[window, window],
        out_specs=[pl.BlockSpec((1,) + shape.shape[1:], lambda g: (g, 0, 0))] * 4,
        out_shape=[shape] * 4,
        name="pack",
        compiler_params=PARAMS,
    )(own, other)


def weights_kernel(u_own, u_other, ph_other, mix_ref, ph_ref):
    kid = pl.program_id(0)
    kids = pl.num_programs(0)
    for i, u in enumerate((u_own, u_other)):
        ur = u[0, 0]
        ui = u[1, 0]
        mix_ref[i * kids + kid, 0] = jnp.concatenate([ur, -ui], axis=0).T
        mix_ref[i * kids + kid, 1] = jnp.concatenate([ui, ur], axis=0).T
    ph_ref[kid] = ph_other[0]


def weights(u_own, u_other, ph_other):
    i, s, b, n = u_own.shape
    _, _, r = ph_other.shape
    kids = s // 2
    window = pl.BlockSpec((i, 1, b, n), lambda g: (0, core() * kids + g, 0, 0))
    return pl.pallas_call(
        weights_kernel,
        grid=(kids,),
        in_specs=[window, window, pl.BlockSpec((1, n, r), lambda g: (core() * kids + g, 0, 0))],
        out_specs=[WHOLE, WHOLE],
        out_shape=[pltpu.VMEM((s, 2, n, 2 * b), BF16), pltpu.VMEM((kids, n, r), BF16)],
        name="weights",
        compiler_params=PARAMS,
    )(u_own, u_other, ph_other)


def band_kernel(line_ref, band_ref):
    def band(row):
        full = jnp.broadcast_to(line_ref[row : row + 1, :], (384, 512))
        return pltpu.roll(full, 448, 1, stride=1, stride_axis=0)[:, :128]

    hr = band(0)
    hi = band(1)
    band_ref[0] = jnp.concatenate([hr, -hi], axis=1).astype(BF16)
    band_ref[1] = jnp.concatenate([hi, hr], axis=1).astype(BF16)


def bands(replica):
    taps = replica.astype(F32)
    line = jnp.concatenate([taps[:, :1], jnp.zeros((2, 383), F32), taps[:, :0:-1]], axis=1)
    return pl.pallas_call(band_kernel, out_shape=jax.ShapeDtypeStruct((2, 384, 256), BF16), name="bands", compiler_params=PARAMS)(line)


def beams_kernel(x_ref, even_ref, odd_ref, band_ref, w_ref, out_ref):
    swath = lax.axis_index("swath")
    odd = (swath & 1) == 1
    even_end = even_ref[...].astype(F32)
    odd_end = odd_ref[...].astype(F32)
    left = jnp.where(swath == 0, 0.0, jnp.where(odd, even_end, odd_end)).astype(BF16)
    right = jnp.where(swath == lax.axis_size("swath") - 1, 0.0, jnp.where(odd, odd_end, even_end)).astype(BF16)
    subs, _, pings, bins = x_ref.shape
    rows = subs * pings
    tiles = bins // 128

    def tile(ri, j):
        return x_ref[:, ri, :, j * 128 : (j + 1) * 128].reshape(rows, 128)

    cre = []
    cim = []
    for j in range(tiles):
        near = [t for t in (j - 1, j, j + 1) if 0 <= t < tiles]
        lhs = [tile(ri, t) for ri in (0, 1) for t in near]
        lo = 128 * (near[0] - j + 1)
        hi = 128 * (near[-1] - j + 2)
        rhs = [band_ref[0, lo:hi], band_ref[1, lo:hi]]
        if j == 0:
            lhs.append(left.reshape(rows, 128))
            rhs += [band_ref[0, 64:128], band_ref[1, 64:128]]
        if j == tiles - 1:
            lhs.append(right.reshape(rows, 128))
            rhs += [band_ref[0, 256:320], band_ref[1, 256:320]]
        c = jnp.dot(jnp.concatenate(lhs, axis=1), jnp.concatenate(rhs, axis=0), preferred_element_type=F32)
        cre.append(c[:, :128].astype(BF16))
        cim.append(c[:, 128:].astype(BF16))
    for s in range(subs):
        part = slice(s * pings, (s + 1) * pings)
        c = jnp.concatenate([jnp.concatenate([t[part] for t in cre], axis=1), jnp.concatenate([t[part] for t in cim], axis=1)], axis=0)
        wr = w_ref[0, s]
        wi = w_ref[1, s]
        out_ref[s, 0] = tdot(jnp.concatenate([wr, -wi], axis=0), c).astype(BF16)
        out_ref[s, 1] = tdot(jnp.concatenate([wi, wr], axis=0), c).astype(BF16)


def beams_of(samples, left, right, band, interp0):
    s, _, _, r = samples.shape
    b = interp0.shape[3]
    return pl.pallas_call(beams_kernel, out_shape=pltpu.VMEM((s, 2, b, r), BF16), name="beams", compiler_params=PARAMS)(
        samples, left, right, band, interp0
    )


def level_kernel(d, mix_ref, ph_own, ph_other, b_own, b_other, out_ref, turn_ref):
    fine = lax.axis_index("fine")
    k = fine & 1
    kids = ph_other.shape[0]
    n = out_ref.shape[1]
    base = pl.multiple_of((((fine >> 1) + d) & 3) * n, n)
    rows = pl.ds(base, n)
    for i, b in enumerate((b_own, b_other)):
        for s in range(kids):
            rhs = b[k * kids + s].reshape(-1, b.shape[3])
            for c in (0, 1):
                turn_ref[i * kids + s, c] = jnp.dot(mix_ref[i * kids + s, c, rows, :], rhs, preferred_element_type=F32)

    step = 16

    def body(j, carry):
        at = pl.ds(pl.multiple_of(j * step, step), step)
        there = pl.ds(pl.multiple_of(base + j * step, step), step)
        re = im = None
        for i, (ph, first) in enumerate(((ph_own, k * kids), (ph_other, 0))):
            for s in range(kids):
                c, t = cos_sin(ph[first + s, there, :].astype(F32))
                tr = turn_ref[i * kids + s, 0, at, :]
                ti = turn_ref[i * kids + s, 1, at, :]
                pr = c * tr - t * ti
                pi = t * tr + c * ti
                re = pr if re is None else re + pr
                im = pi if im is None else im + pi
        out_ref[0, at, :] = re.astype(out_ref.dtype)
        out_ref[1, at, :] = im.astype(out_ref.dtype)
        return carry

    lax.fori_loop(0, n // step, body, 0)


def level_part(d, dtype, *operands):
    mix, ph = operands[:2]
    s, _, n, _ = mix.shape
    n //= 4
    r = ph.shape[2]
    return pl.pallas_call(
        lambda *refs: level_kernel(d, *refs),
        in_specs=[WHOLE] * 5,
        out_specs=WHOLE,
        scratch_shapes=[pltpu.VMEM((s, 2, n, r), F32)],
        out_shape=pltpu.VMEM((2, n, r), dtype),
        name="level",
        compiler_params=PARAMS,
    )(*[near(x) for x in operands])


def turn_kernel(ph_ref, out_ref):
    step = 16

    def body(j, carry):
        at = pl.ds(pl.multiple_of(j * step, step), step)
        c, s = cos_sin(ph_ref[at, :].astype(F32))
        out_ref[0, at, :] = c
        out_ref[1, at, :] = s
        return carry

    lax.fori_loop(0, ph_ref.shape[0] // step, body, 0)


def turns(ph):
    return pl.pallas_call(
        turn_kernel,
        in_specs=[WHOLE],
        out_specs=WHOLE,
        out_shape=pltpu.VMEM((2,) + ph.shape, F32),
        name="turns",
        compiler_params=PARAMS,
    )(near(ph))


def mixed(us, vs, i):
    lhs = [x for u in us for x in ((u[0], -u[1]) if i == 0 else (u[1], u[0]))]
    rhs = [v[j] for v in vs for j in (0, 1)]
    return tdot(jnp.concatenate(lhs, axis=0), jnp.concatenate(rhs, axis=0))


def gather_kernel(*refs):
    half = len(refs) // 2
    for i in (0, 1):
        refs[-1][i] = mixed(refs[:half], refs[half:-1], i)


def gathered(us, vs):
    _, _, m = us[0].shape
    _, _, r = vs[0].shape
    return pl.pallas_call(
        gather_kernel,
        in_specs=[WHOLE] * (2 * len(us)),
        out_specs=WHOLE,
        out_shape=pltpu.VMEM((2, m, r), F32),
        name="gathered",
        compiler_params=PARAMS,
    )(*[near(x) for x in us], *[near(x) for x in vs])


def image_kernel(u_ref, v_ref, part_ref, turn_ref, keep_ref, send_ref, acc_ref):
    own = core() == 0
    for i in (0, 1):
        acc_ref[i] = part_ref[i] + mixed((u_ref,), (v_ref,), i)

    def body(c, carry):
        x = c & 3
        z = c >> 2
        halves = []
        for h in (0, 1):
            at = pl.ds(pl.multiple_of(c * 64 + h * 32, 32), 32)
            co = turn_ref[0, at, :]
            si = turn_ref[1, at, :]
            re = acc_ref[0, at, :]
            im = acc_ref[1, at, :]
            halves.append((co * re - si * im, si * re + co * im))
        for i in (0, 1):
            keep_ref[x, z, i] = jnp.where(own, halves[0][i], halves[1][i])
            send_ref[x, z, i] = jnp.where(own, halves[1][i], halves[0][i]).astype(BF16)
        return carry

    lax.fori_loop(0, 8, body, 0)


def image_parts(u, v, part, turn):
    _, m, r = turn.shape
    shape = (4, 2, 2, m // 16, r)
    return pl.pallas_call(
        image_kernel,
        in_specs=[WHOLE] * 4,
        out_specs=[WHOLE, WHOLE],
        scratch_shapes=[pltpu.VMEM((2, m, r), F32)],
        out_shape=[pltpu.VMEM(shape, F32), pltpu.VMEM(shape, BF16)],
        name="image",
        compiler_params=PARAMS,
    )(near(u), near(v), near(part), near(turn))


def join_kernel(*refs):
    total = refs[0][...]
    for ref in refs[1:-1]:
        total += ref[...].astype(F32)
    refs[-1][...] = total.astype(BF16)


def join(first, *rest):
    return pl.pallas_call(
        join_kernel,
        in_specs=[WHOLE] * (1 + len(rest)),
        out_specs=WHOLE,
        out_shape=pltpu.VMEM(first.shape, BF16),
        name="join",
        compiler_params=PARAMS,
    )(*[near(x) for x in (first,) + rest])


def finish_kernel(*refs):
    for i in (0, 1):
        total = refs[0][i]
        for ref in refs[1:-1]:
            total += ref[i].astype(F32)
        refs[-1][:, i, :] = total


def finish(first, *rest):
    i, m, r = first.shape
    return pl.pallas_call(
        finish_kernel,
        in_specs=[WHOLE] * (1 + len(rest)),
        out_specs=WHOLE,
        out_shape=jax.ShapeDtypeStruct((m, i, r), F32),
        name="finish",
        compiler_params=PARAMS,
    )(*[near(x) for x in (first,) + rest])


def program(echoes, exponents, replica, interp0, upsample1, phase1, upsample2, phase2):
    fine = lax.axis_index("fine")
    coarse = lax.axis_index("coarse")
    y = fine // 2
    k = fine % 2
    cx = coarse % 4
    cz = coarse // 4
    range_bins = echoes.shape[3]

    expo = jnp.transpose(exponents, (0, 2, 1))
    u2_other = swap_cores(upsample2)
    u1_other = swap_cores(upsample1)
    even, odd = ends(echoes, expo)
    even = lax.ppermute(even, "swath", [(0, 1), (1, 0), (2, 3), (3, 2)])
    odd = lax.ppermute(odd, "swath", [(0, 0), (1, 2), (2, 1), (3, 3)])
    ph_own = jnp.transpose(phase1, (1, 0, 2))
    ph_other = swap_cores(ph_own)
    band = bands(replica)
    u2_parts = pack(upsample2, u2_other)
    samples = prep(echoes, expo)
    u2_parts = [u2_parts[0]] + [shift_chips(u2_parts[d], d) for d in (1, 2, 3)]

    b_own = beams_of(samples, even, odd, band, interp0)
    b_other = swap_cores(b_own)

    mix, ph_other = weights(upsample1, u1_other, ph_other)
    operands = (mix, ph_own, ph_other, b_own, b_other)
    received = [shift_chips(level_part(d, BF16, *operands), d) for d in (2, 1, 3)]
    total = level_part(0, F32, *operands)
    for part in received:
        total += part.astype(F32)
    level = total.astype(BF16)
    levels = [level] + [shift_chips(level, d) for d in (1, 2, 3)]

    ph2 = pick(pick(phase2.reshape(8, 4, 64, 2, range_bins), y, 1), k, 2).reshape(512, range_bins)
    turn = turns(ph2)

    keep, send = image_parts(u2_parts[3], levels[3], gathered(u2_parts[:3], levels[:3]), turn)
    other = swap_cores(send)
    narrow = (keep + other.astype(F32)).astype(BF16)

    def shares(z):
        first = pick(pick(keep, cx), z) + pick(pick(other, cx), z).astype(F32)
        return [first] + [shift_x(pick(pick(narrow, (cx + d) % 4), z), d) for d in (2, 1, 3)]

    far = swap_z(join(*shares(1 - cz)))
    return finish(*shares(cz), far)


def solution(mesh):
    in_specs = (
        P(("coarse", "fine"), None, None, "swath"),
        P(("coarse", "fine"), None, "swath"),
        P(),
        P(None, ("coarse", "fine"), None, None),
        P(None, ("coarse", "fine"), None, None),
        P(None, ("coarse", "fine"), "swath"),
        P("coarse", None, "fine", None),
        P(None, "coarse", "swath"),
    )
    out_specs = P(("coarse", "fine"), None, "swath")
    return jax.shard_map(program, mesh=mesh, in_specs=in_specs, out_specs=out_specs, check_vma=False)
```

```python
import jax
import jax.numpy as jnp
from jax import lax
from jax.experimental import pallas as pl
from jax.experimental.pallas import tpu as pltpu
from jax.sharding import PartitionSpec as P


F32 = jnp.float32
BF16 = jnp.bfloat16

SIN = (0.7071067690849304, -0.029462749138474464, 0.0003682656097225845, -2.1877108338230755e-06, 7.155278591852721e-09)
COS = (1.4142135381698608, -0.17677636444568634, 0.003682575421407819, -3.061265670112334e-05, 1.279087769034959e-07)
VMEM = pltpu.MemorySpace.VMEM
PARAMS = pltpu.CompilerParams(vmem_limit_bytes=16 << 20)
WHOLE = pl.BlockSpec(memory_space=pltpu.MemorySpace.VMEM)


def horner(u, coefs):
    total = coefs[-1] * u + coefs[-2]
    for c in coefs[-3::-1]:
        total = total * u + c
    return total


def cos_sin(x):
    u = x * x
    s = x * horner(u, SIN)
    return 1.0 - s * s, s * horner(u, COS)


def near(x):
    return pltpu.with_memory_space_constraint(x, VMEM)


def swap_cores(x):
    return lax.ppermute(x, "fine", [(i, i ^ 1) for i in range(8)])


def shift_chips(x, d):
    return lax.ppermute(x, "fine", [(y * 2 + k, (y + d) % 4 * 2 + k) for y in range(4) for k in range(2)])


def shift_x(x, d):
    return lax.ppermute(x, "coarse", [(z * 4 + i, z * 4 + (i + d) % 4) for z in range(2) for i in range(4)])


def swap_z(x):
    return lax.ppermute(x, "coarse", [(i, i ^ 4) for i in range(8)])


def pick(x, i, axis=0):
    return lax.dynamic_index_in_dim(x, i, axis, keepdims=False)


def tdot(a, b):
    return lax.dot_general(a, b, (((0,), (0,)), ((), ())), preferred_element_type=F32)


def factors(expo, lo, lanes):
    blocks = expo.shape[0]
    bins = lo + lax.broadcasted_iota(jnp.int32, (blocks, lanes), 1)
    expand = bins // 32 == lax.broadcasted_iota(jnp.int32, (blocks, lanes), 0)
    scale = (jnp.left_shift(1, expo).astype(F32) * (1.0 / 256.0)).astype(BF16)
    return tdot(scale, expand.astype(F32).astype(BF16))


def ends_kernel(low_ref, high_ref, expo_ref, even_ref, odd_ref):
    odd = (lax.axis_index("swath") & 1) == 1
    subs, pings, _, lanes = low_ref.shape
    low = lax.broadcasted_iota(jnp.int32, (pings, lanes), 1) < 64
    start = 32 * expo_ref.shape[1] - lanes
    for s in range(subs):
        factor = factors(expo_ref[s], 0, lanes)
        re = low_ref[s, :, 0, :].astype(F32) * factor
        im = low_ref[s, :, 1, :].astype(F32) * factor
        first = jnp.where(low, re, pltpu.roll(im, 64, 1))
        factor = factors(expo_ref[s], start, lanes)
        re = high_ref[s, :, 0, :].astype(F32) * factor
        im = high_ref[s, :, 1, :].astype(F32) * factor
        last = jnp.where(low, pltpu.roll(re, 64, 1), im)
        even_ref[s] = jnp.where(odd, first, last).astype(BF16)
        odd_ref[s] = jnp.where(odd, last, first).astype(BF16)


def ends(echoes, exponents):
    s, l, _, r = echoes.shape
    b = exponents.shape[1]
    shape = jax.ShapeDtypeStruct((s, l, 128), BF16)
    whole = pl.BlockSpec((s, l, 128), lambda i: (0, 0, 0))
    return pl.pallas_call(
        ends_kernel,
        grid=(1,),
        in_specs=[
            pl.BlockSpec((s, l, 2, 128), lambda i: (0, 0, 0, 0)),
            pl.BlockSpec((s, l, 2, 128), lambda i: (0, 0, 0, r // 128 - 1)),
            pl.BlockSpec((s, b, l), lambda i: (0, 0, 0)),
        ],
        out_specs=[whole, whole],
        out_shape=[shape, shape],
        name="ends",
        compiler_params=PARAMS,
    )(echoes, echoes, exponents)


def prep_kernel(echo_ref, expo_ref, out_ref):
    for s in range(echo_ref.shape[0]):
        factor = factors(expo_ref[s], 0, echo_ref.shape[3])
        for i in (0, 1):
            out_ref[s, i] = (echo_ref[s, :, i, :].astype(F32) * factor).astype(BF16)


def prep(echoes, exponents):
    s, l, _, r = echoes.shape
    b = exponents.shape[1]
    return pl.pallas_call(
        prep_kernel,
        grid=(2,),
        in_specs=[
            pl.BlockSpec((s // 2, l, 2, r), lambda i: (i, 0, 0, 0)),
            pl.BlockSpec((s // 2, b, l), lambda i: (i, 0, 0)),
        ],
        out_specs=pl.BlockSpec((s // 2, 2, l, r), lambda i: (i, 0, 0, 0)),
        out_shape=jax.ShapeDtypeStruct((s, 2, l, r), BF16),
        name="prep",
        compiler_params=PARAMS,
    )(echoes, exponents)


def core():
    return lax.axis_index("fine") & 1


def pack_kernel(own_ref, other_ref, *out_refs):
    fine = lax.axis_index("fine")
    k = fine & 1
    rows = own_ref.shape[2]
    low = lax.broadcasted_iota(jnp.int32, (rows, 128), 1) < 64
    for d, out in enumerate(out_refs):
        y = ((fine >> 1) + d) & 3
        even = (y & 1) == 0
        base = pl.multiple_of((y >> 1) * 128, 128)
        for ref, half in ((own_ref, k), (other_ref, 1 - k)):
            at = pl.ds(pl.multiple_of(half * rows, rows), rows)
            for p in range(4):
                a = ref[0, 0, :, pl.ds(base + p * 512, 128)].astype(F32)
                b = ref[0, 0, :, pl.ds(base + p * 512 + 256, 128)].astype(F32)
                c = pltpu.roll(jnp.where(even, b, a), 64, 1)
                out[0, at, p * 128 : (p + 1) * 128] = jnp.where(low, jnp.where(even, a, c), jnp.where(even, c, b)).astype(BF16)


def pack(own, other):
    _, i, rows, m = own.shape
    shape = jax.ShapeDtypeStruct((2, 2 * rows, m // 4), BF16)
    window = pl.BlockSpec((1, 1, rows, m), lambda g: (core(), g, 0, 0))
    return pl.pallas_call(
        pack_kernel,
        grid=(i,),
        in_specs=[window, window],
        out_specs=[pl.BlockSpec((1,) + shape.shape[1:], lambda g: (g, 0, 0))] * 4,
        out_shape=[shape] * 4,
        name="pack",
        compiler_params=PARAMS,
    )(own, other)


def weights_kernel(u_own, u_other, ph_other, mix_ref, ph_ref):
    kid = pl.program_id(0)
    kids = pl.num_programs(0)
    for i, u in enumerate((u_own, u_other)):
        ur = u[0, 0]
        ui = u[1, 0]
        mix_ref[i * kids + kid, 0] = jnp.concatenate([ur, -ui], axis=0).T
        mix_ref[i * kids + kid, 1] = jnp.concatenate([ui, ur], axis=0).T
    ph_ref[kid] = ph_other[0]


def weights(u_own, u_other, ph_other):
    i, s, b, n = u_own.shape
    _, _, r = ph_other.shape
    kids = s // 2
    window = pl.BlockSpec((i, 1, b, n), lambda g: (0, core() * kids + g, 0, 0))
    return pl.pallas_call(
        weights_kernel,
        grid=(kids,),
        in_specs=[window, window, pl.BlockSpec((1, n, r), lambda g: (core() * kids + g, 0, 0))],
        out_specs=[WHOLE, WHOLE],
        out_shape=[pltpu.VMEM((s, 2, n, 2 * b), BF16), pltpu.VMEM((kids, n, r), BF16)],
        name="weights",
        compiler_params=PARAMS,
    )(u_own, u_other, ph_other)


def band_kernel(line_ref, band_ref):
    def band(row):
        full = jnp.broadcast_to(line_ref[row : row + 1, :], (384, 512))
        return pltpu.roll(full, 448, 1, stride=1, stride_axis=0)[:, :128]

    hr = band(0)
    hi = band(1)
    band_ref[0] = jnp.concatenate([hr, -hi], axis=1).astype(BF16)
    band_ref[1] = jnp.concatenate([hi, hr], axis=1).astype(BF16)


def bands(replica):
    taps = replica.astype(F32)
    line = jnp.concatenate([taps[:, :1], jnp.zeros((2, 383), F32), taps[:, :0:-1]], axis=1)
    return pl.pallas_call(band_kernel, out_shape=jax.ShapeDtypeStruct((2, 384, 256), BF16), name="bands", compiler_params=PARAMS)(line)


def beams_kernel(x_ref, even_ref, odd_ref, band_ref, w_ref, out_ref):
    swath = lax.axis_index("swath")
    odd = (swath & 1) == 1
    even_end = even_ref[...].astype(F32)
    odd_end = odd_ref[...].astype(F32)
    left = jnp.where(swath == 0, 0.0, jnp.where(odd, even_end, odd_end)).astype(BF16)
    right = jnp.where(swath == lax.axis_size("swath") - 1, 0.0, jnp.where(odd, odd_end, even_end)).astype(BF16)
    subs, _, pings, bins = x_ref.shape
    rows = subs * pings
    tiles = bins // 128

    def tile(ri, j):
        return x_ref[:, ri, :, j * 128 : (j + 1) * 128].reshape(rows, 128)

    cre = []
    cim = []
    for j in range(tiles):
        near = [t for t in (j - 1, j, j + 1) if 0 <= t < tiles]
        lhs = [tile(ri, t) for ri in (0, 1) for t in near]
        lo = 128 * (near[0] - j + 1)
        hi = 128 * (near[-1] - j + 2)
        rhs = [band_ref[0, lo:hi], band_ref[1, lo:hi]]
        if j == 0:
            lhs.append(left.reshape(rows, 128))
            rhs += [band_ref[0, 64:128], band_ref[1, 64:128]]
        if j == tiles - 1:
            lhs.append(right.reshape(rows, 128))
            rhs += [band_ref[0, 256:320], band_ref[1, 256:320]]
        c = jnp.dot(jnp.concatenate(lhs, axis=1), jnp.concatenate(rhs, axis=0), preferred_element_type=F32)
        cre.append(c[:, :128].astype(BF16))
        cim.append(c[:, 128:].astype(BF16))
    for s in range(subs):
        part = slice(s * pings, (s + 1) * pings)
        c = jnp.concatenate([jnp.concatenate([t[part] for t in cre], axis=1), jnp.concatenate([t[part] for t in cim], axis=1)], axis=0)
        wr = w_ref[0, s]
        wi = w_ref[1, s]
        out_ref[s, 0] = tdot(jnp.concatenate([wr, -wi], axis=0), c).astype(BF16)
        out_ref[s, 1] = tdot(jnp.concatenate([wi, wr], axis=0), c).astype(BF16)


def beams_of(samples, left, right, band, interp0):
    s, _, _, r = samples.shape
    b = interp0.shape[3]
    return pl.pallas_call(beams_kernel, out_shape=pltpu.VMEM((s, 2, b, r), BF16), name="beams", compiler_params=PARAMS)(
        samples, left, right, band, interp0
    )


def level_kernel(d, mix_ref, ph_own, ph_other, b_own, b_other, out_ref, turn_ref):
    fine = lax.axis_index("fine")
    k = fine & 1
    kids = ph_other.shape[0]
    n = out_ref.shape[1]
    base = pl.multiple_of((((fine >> 1) + d) & 3) * n, n)
    rows = pl.ds(base, n)
    for i, b in enumerate((b_own, b_other)):
        for s in range(kids):
            rhs = b[k * kids + s].reshape(-1, b.shape[3])
            for c in (0, 1):
                turn_ref[i * kids + s, c] = jnp.dot(mix_ref[i * kids + s, c, rows, :], rhs, preferred_element_type=F32)

    step = 16

    def body(j, carry):
        at = pl.ds(pl.multiple_of(j * step, step), step)
        there = pl.ds(pl.multiple_of(base + j * step, step), step)
        re = im = None
        for i, (ph, first) in enumerate(((ph_own, k * kids), (ph_other, 0))):
            for s in range(kids):
                c, t = cos_sin(ph[first + s, there, :].astype(F32))
                tr = turn_ref[i * kids + s, 0, at, :]
                ti = turn_ref[i * kids + s, 1, at, :]
                pr = c * tr - t * ti
                pi = t * tr + c * ti
                re = pr if re is None else re + pr
                im = pi if im is None else im + pi
        out_ref[0, at, :] = re.astype(out_ref.dtype)
        out_ref[1, at, :] = im.astype(out_ref.dtype)
        return carry

    lax.fori_loop(0, n // step, body, 0)


def level_part(d, dtype, *operands):
    mix, ph = operands[:2]
    s, _, n, _ = mix.shape
    n //= 4
    r = ph.shape[2]
    return pl.pallas_call(
        lambda *refs: level_kernel(d, *refs),
        in_specs=[WHOLE] * 5,
        out_specs=WHOLE,
        scratch_shapes=[pltpu.VMEM((s, 2, n, r), F32)],
        out_shape=pltpu.VMEM((2, n, r), dtype),
        name="level",
        compiler_params=PARAMS,
    )(*[near(x) for x in operands])


def turn_kernel(ph_ref, out_ref):
    step = 16

    def body(j, carry):
        at = pl.ds(pl.multiple_of(j * step, step), step)
        c, s = cos_sin(ph_ref[at, :].astype(F32))
        out_ref[0, at, :] = c
        out_ref[1, at, :] = s
        return carry

    lax.fori_loop(0, ph_ref.shape[0] // step, body, 0)


def turns(ph):
    return pl.pallas_call(
        turn_kernel,
        in_specs=[WHOLE],
        out_specs=WHOLE,
        out_shape=pltpu.VMEM((2,) + ph.shape, F32),
        name="turns",
        compiler_params=PARAMS,
    )(near(ph))


def mixed(us, vs, i):
    lhs = [x for u in us for x in ((u[0], -u[1]) if i == 0 else (u[1], u[0]))]
    rhs = [v[j] for v in vs for j in (0, 1)]
    return tdot(jnp.concatenate(lhs, axis=0), jnp.concatenate(rhs, axis=0))


def gather_kernel(*refs):
    half = len(refs) // 2
    for i in (0, 1):
        refs[-1][i] = mixed(refs[:half], refs[half:-1], i)


def gathered(us, vs):
    _, _, m = us[0].shape
    _, _, r = vs[0].shape
    return pl.pallas_call(
        gather_kernel,
        in_specs=[WHOLE] * (2 * len(us)),
        out_specs=WHOLE,
        out_shape=pltpu.VMEM((2, m, r), F32),
        name="gathered",
        compiler_params=PARAMS,
    )(*[near(x) for x in us], *[near(x) for x in vs])


def image_kernel(u_ref, low_ref, high_ref, part_ref, turn_ref, keep_ref, send_ref, acc_ref):
    own = core() == 0
    v = [jnp.concatenate([low_ref[j], high_ref[j]], axis=0) for j in (0, 1)]
    for i in (0, 1):
        acc_ref[i] = part_ref[i] + mixed((u_ref,), (v,), i)

    def body(c, carry):
        x = c & 3
        z = c >> 2
        halves = []
        for h in (0, 1):
            at = pl.ds(pl.multiple_of(c * 64 + h * 32, 32), 32)
            co = turn_ref[0, at, :]
            si = turn_ref[1, at, :]
            re = acc_ref[0, at, :]
            im = acc_ref[1, at, :]
            halves.append((co * re - si * im, si * re + co * im))
        for i in (0, 1):
            keep_ref[x, z, i] = jnp.where(own, halves[0][i], halves[1][i])
            send_ref[x, z, i] = jnp.where(own, halves[1][i], halves[0][i]).astype(BF16)
        return carry

    lax.fori_loop(0, 8, body, 0)


def image_parts(u, low, high, part, turn):
    _, m, r = turn.shape
    shape = (4, 2, 2, m // 16, r)
    return pl.pallas_call(
        image_kernel,
        in_specs=[WHOLE] * 5,
        out_specs=[WHOLE, WHOLE],
        scratch_shapes=[pltpu.VMEM((2, m, r), F32)],
        out_shape=[pltpu.VMEM(shape, F32), pltpu.VMEM(shape, BF16)],
        name="image",
        compiler_params=PARAMS,
    )(near(u), near(low), near(high), near(part), near(turn))


def join_kernel(*refs):
    total = refs[0][...]
    for ref in refs[1:-1]:
        total += ref[...].astype(F32)
    refs[-1][...] = total.astype(BF16)


def join(first, *rest):
    return pl.pallas_call(
        join_kernel,
        in_specs=[WHOLE] * (1 + len(rest)),
        out_specs=WHOLE,
        out_shape=pltpu.VMEM(first.shape, BF16),
        name="join",
        compiler_params=PARAMS,
    )(*[near(x) for x in (first,) + rest])


def finish_kernel(*refs):
    for i in (0, 1):
        total = refs[0][i]
        for ref in refs[1:-1]:
            total += ref[i].astype(F32)
        refs[-1][:, i, :] = total


def finish(first, *rest):
    i, m, r = first.shape
    return pl.pallas_call(
        finish_kernel,
        in_specs=[WHOLE] * (1 + len(rest)),
        out_specs=WHOLE,
        out_shape=jax.ShapeDtypeStruct((m, i, r), F32),
        name="finish",
        compiler_params=PARAMS,
    )(*[near(x) for x in (first,) + rest])


def program(echoes, exponents, replica, interp0, upsample1, phase1, upsample2, phase2):
    fine = lax.axis_index("fine")
    coarse = lax.axis_index("coarse")
    y = fine // 2
    k = fine % 2
    cx = coarse % 4
    cz = coarse // 4
    range_bins = echoes.shape[3]

    expo = jnp.transpose(exponents, (0, 2, 1))
    u2_other = swap_cores(upsample2)
    u1_other = swap_cores(upsample1)
    even, odd = ends(echoes, expo)
    even = lax.ppermute(even, "swath", [(0, 1), (1, 0), (2, 3), (3, 2)])
    odd = lax.ppermute(odd, "swath", [(0, 0), (1, 2), (2, 1), (3, 3)])
    ph_own = jnp.transpose(phase1, (1, 0, 2))
    ph_other = swap_cores(ph_own)
    band = bands(replica)
    u2_parts = pack(upsample2, u2_other)
    samples = prep(echoes, expo)
    u2_parts = [u2_parts[0]] + [shift_chips(u2_parts[d], d) for d in (1, 2, 3)]

    b_own = beams_of(samples, even, odd, band, interp0)
    b_other = swap_cores(b_own)

    mix, ph_other = weights(upsample1, u1_other, ph_other)
    operands = (mix, ph_own, ph_other, b_own, b_other)
    received = [shift_chips(level_part(d, BF16, *operands), d) for d in (2, 1, 3)]
    total = level_part(0, F32, *operands)
    for part in received:
        total += part.astype(F32)
    level = total.astype(BF16)
    before = shift_chips(level, 1)
    after = shift_chips(level, 3)
    half = level.shape[1] // 2
    low = shift_chips(before[:, :half], 1)
    high = shift_chips(after[:, half:], 3)

    ph2 = pick(pick(phase2.reshape(8, 4, 64, 2, range_bins), y, 1), k, 2).reshape(512, range_bins)
    turn = turns(ph2)

    keep, send = image_parts(
        u2_parts[2], low, high, gathered([u2_parts[0], u2_parts[1], u2_parts[3]], [level, before, after]), turn
    )
    other = swap_cores(send)
    narrow = (keep + other.astype(F32)).astype(BF16)

    def shares(z):
        first = pick(pick(keep, cx), z) + pick(pick(other, cx), z).astype(F32)
        return [first] + [shift_x(pick(pick(narrow, (cx + d) % 4), z), d) for d in (2, 1, 3)]

    far = swap_z(join(*shares(1 - cz)))
    return finish(*shares(cz), far)


def solution(mesh):
    in_specs = (
        P(("coarse", "fine"), None, None, "swath"),
        P(("coarse", "fine"), None, "swath"),
        P(),
        P(None, ("coarse", "fine"), None, None),
        P(None, ("coarse", "fine"), None, None),
        P(None, ("coarse", "fine"), "swath"),
        P("coarse", None, "fine", None),
        P(None, "coarse", "swath"),
    )
    out_specs = P(("coarse", "fine"), None, "swath")
    return jax.shard_map(program, mesh=mesh, in_specs=in_specs, out_specs=out_specs, check_vma=False)
```

```python
import jax
import jax.numpy as jnp
from jax import lax
from jax.experimental import pallas as pl
from jax.experimental.pallas import tpu as pltpu
from jax.sharding import PartitionSpec as P


F32 = jnp.float32
BF16 = jnp.bfloat16

SIN = (0.7071067690849304, -0.029462749138474464, 0.0003682656097225845, -2.1877108338230755e-06, 7.155278591852721e-09)
COS = (1.4142135381698608, -0.17677636444568634, 0.003682575421407819, -3.061265670112334e-05, 1.279087769034959e-07)
VMEM = pltpu.MemorySpace.VMEM
PARAMS = pltpu.CompilerParams(vmem_limit_bytes=16 << 20)
WHOLE = pl.BlockSpec(memory_space=pltpu.MemorySpace.VMEM)


def horner(u, coefs):
    total = coefs[-1] * u + coefs[-2]
    for c in coefs[-3::-1]:
        total = total * u + c
    return total


def cos_sin(x):
    u = x * x
    s = x * horner(u, SIN)
    return 1.0 - s * s, s * horner(u, COS)


def near(x):
    return pltpu.with_memory_space_constraint(x, VMEM)


def swap_cores(x):
    return lax.ppermute(x, "fine", [(i, i ^ 1) for i in range(8)])


def shift_chips(x, d):
    return lax.ppermute(x, "fine", [(y * 2 + k, (y + d) % 4 * 2 + k) for y in range(4) for k in range(2)])


def shift_x(x, d):
    return lax.ppermute(x, "coarse", [(z * 4 + i, z * 4 + (i + d) % 4) for z in range(2) for i in range(4)])


def swap_z(x):
    return lax.ppermute(x, "coarse", [(i, i ^ 4) for i in range(8)])


def pick(x, i, axis=0):
    return lax.dynamic_index_in_dim(x, i, axis, keepdims=False)


def tdot(a, b):
    return lax.dot_general(a, b, (((0,), (0,)), ((), ())), preferred_element_type=F32)


def factors(expo, lo, lanes):
    blocks = expo.shape[0]
    bins = lo + lax.broadcasted_iota(jnp.int32, (blocks, lanes), 1)
    expand = bins // 32 == lax.broadcasted_iota(jnp.int32, (blocks, lanes), 0)
    scale = (jnp.left_shift(1, expo).astype(F32) * (1.0 / 256.0)).astype(BF16)
    return tdot(scale, expand.astype(F32).astype(BF16))


def ends_kernel(low_ref, high_ref, expo_ref, even_ref, odd_ref):
    odd = (lax.axis_index("swath") & 1) == 1
    subs, pings, _, lanes = low_ref.shape
    low = lax.broadcasted_iota(jnp.int32, (pings, lanes), 1) < 64
    start = 32 * expo_ref.shape[1] - lanes
    for s in range(subs):
        factor = factors(expo_ref[s], 0, lanes)
        re = low_ref[s, :, 0, :].astype(F32) * factor
        im = low_ref[s, :, 1, :].astype(F32) * factor
        first = jnp.where(low, re, pltpu.roll(im, 64, 1))
        factor = factors(expo_ref[s], start, lanes)
        re = high_ref[s, :, 0, :].astype(F32) * factor
        im = high_ref[s, :, 1, :].astype(F32) * factor
        last = jnp.where(low, pltpu.roll(re, 64, 1), im)
        even_ref[s] = jnp.where(odd, first, last).astype(BF16)
        odd_ref[s] = jnp.where(odd, last, first).astype(BF16)


def ends(echoes, exponents):
    s, l, _, r = echoes.shape
    b = exponents.shape[1]
    shape = jax.ShapeDtypeStruct((s, l, 128), BF16)
    whole = pl.BlockSpec((s, l, 128), lambda i: (0, 0, 0))
    return pl.pallas_call(
        ends_kernel,
        grid=(1,),
        in_specs=[
            pl.BlockSpec((s, l, 2, 128), lambda i: (0, 0, 0, 0)),
            pl.BlockSpec((s, l, 2, 128), lambda i: (0, 0, 0, r // 128 - 1)),
            pl.BlockSpec((s, b, l), lambda i: (0, 0, 0)),
        ],
        out_specs=[whole, whole],
        out_shape=[shape, shape],
        name="ends",
        compiler_params=PARAMS,
    )(echoes, echoes, exponents)


def prep_kernel(echo_ref, expo_ref, out_ref):
    for s in range(echo_ref.shape[0]):
        factor = factors(expo_ref[s], 0, echo_ref.shape[3])
        for i in (0, 1):
            out_ref[s, i] = (echo_ref[s, :, i, :].astype(F32) * factor).astype(BF16)


def prep(echoes, exponents):
    s, l, _, r = echoes.shape
    b = exponents.shape[1]
    return pl.pallas_call(
        prep_kernel,
        grid=(2,),
        in_specs=[
            pl.BlockSpec((s // 2, l, 2, r), lambda i: (i, 0, 0, 0)),
            pl.BlockSpec((s // 2, b, l), lambda i: (i, 0, 0)),
        ],
        out_specs=pl.BlockSpec((s // 2, 2, l, r), lambda i: (i, 0, 0, 0)),
        out_shape=jax.ShapeDtypeStruct((s, 2, l, r), BF16),
        name="prep",
        compiler_params=PARAMS,
    )(echoes, exponents)


def core():
    return lax.axis_index("fine") & 1


def pack_kernel(shifts, own_ref, other_ref, *out_refs):
    fine = lax.axis_index("fine")
    k = fine & 1
    rows = own_ref.shape[2]
    low = lax.broadcasted_iota(jnp.int32, (rows, 128), 1) < 64
    for d, out in zip(shifts, out_refs):
        y = ((fine >> 1) + d) & 3
        even = (y & 1) == 0
        base = pl.multiple_of((y >> 1) * 128, 128)
        for ref, half in ((own_ref, k), (other_ref, 1 - k)):
            at = pl.ds(pl.multiple_of(half * rows, rows), rows)
            for p in range(4):
                a = ref[0, 0, :, pl.ds(base + p * 512, 128)].astype(F32)
                b = ref[0, 0, :, pl.ds(base + p * 512 + 256, 128)].astype(F32)
                c = pltpu.roll(jnp.where(even, b, a), 64, 1)
                out[0, at, p * 128 : (p + 1) * 128] = jnp.where(low, jnp.where(even, a, c), jnp.where(even, c, b)).astype(BF16)


def pack(shifts, own, other):
    _, i, rows, m = own.shape
    shape = jax.ShapeDtypeStruct((2, 2 * rows, m // 4), BF16)
    window = pl.BlockSpec((1, 1, rows, m), lambda g: (core(), g, 0, 0))
    return pl.pallas_call(
        lambda *refs: pack_kernel(shifts, *refs),
        grid=(i,),
        in_specs=[window, window],
        out_specs=[pl.BlockSpec((1,) + shape.shape[1:], lambda g: (g, 0, 0))] * len(shifts),
        out_shape=[shape] * len(shifts),
        name="pack",
        compiler_params=PARAMS,
    )(own, other)


def weights_kernel(u_own, u_other, ph_other, mix_ref, ph_ref):
    kid = pl.program_id(0)
    kids = pl.num_programs(0)
    for i, u in enumerate((u_own, u_other)):
        ur = u[0, 0]
        ui = u[1, 0]
        mix_ref[i * kids + kid, 0] = jnp.concatenate([ur, -ui], axis=0).T
        mix_ref[i * kids + kid, 1] = jnp.concatenate([ui, ur], axis=0).T
    ph_ref[kid] = ph_other[0]


def weights(u_own, u_other, ph_other):
    i, s, b, n = u_own.shape
    _, _, r = ph_other.shape
    kids = s // 2
    window = pl.BlockSpec((i, 1, b, n), lambda g: (0, core() * kids + g, 0, 0))
    return pl.pallas_call(
        weights_kernel,
        grid=(kids,),
        in_specs=[window, window, pl.BlockSpec((1, n, r), lambda g: (core() * kids + g, 0, 0))],
        out_specs=[WHOLE, WHOLE],
        out_shape=[pltpu.VMEM((s, 2, n, 2 * b), BF16), pltpu.VMEM((kids, n, r), BF16)],
        name="weights",
        compiler_params=PARAMS,
    )(u_own, u_other, ph_other)


def band_kernel(line_ref, band_ref):
    def band(row):
        full = jnp.broadcast_to(line_ref[row : row + 1, :], (384, 512))
        return pltpu.roll(full, 448, 1, stride=1, stride_axis=0)[:, :128]

    hr = band(0)
    hi = band(1)
    band_ref[0] = jnp.concatenate([hr, -hi], axis=1).astype(BF16)
    band_ref[1] = jnp.concatenate([hi, hr], axis=1).astype(BF16)


def bands(replica):
    taps = replica.astype(F32)
    line = jnp.concatenate([taps[:, :1], jnp.zeros((2, 383), F32), taps[:, :0:-1]], axis=1)
    return pl.pallas_call(band_kernel, out_shape=jax.ShapeDtypeStruct((2, 384, 256), BF16), name="bands", compiler_params=PARAMS)(line)


def beams_kernel(x_ref, even_ref, odd_ref, band_ref, w_ref, out_ref):
    swath = lax.axis_index("swath")
    odd = (swath & 1) == 1
    even_end = even_ref[...].astype(F32)
    odd_end = odd_ref[...].astype(F32)
    left = jnp.where(swath == 0, 0.0, jnp.where(odd, even_end, odd_end)).astype(BF16)
    right = jnp.where(swath == lax.axis_size("swath") - 1, 0.0, jnp.where(odd, odd_end, even_end)).astype(BF16)
    subs, _, pings, bins = x_ref.shape
    rows = subs * pings
    tiles = bins // 128

    def tile(ri, j):
        return x_ref[:, ri, :, j * 128 : (j + 1) * 128].reshape(rows, 128)

    cre = []
    cim = []
    for j in range(tiles):
        near = [t for t in (j - 1, j, j + 1) if 0 <= t < tiles]
        lhs = [tile(ri, t) for ri in (0, 1) for t in near]
        lo = 128 * (near[0] - j + 1)
        hi = 128 * (near[-1] - j + 2)
        rhs = [band_ref[0, lo:hi], band_ref[1, lo:hi]]
        if j == 0:
            lhs.append(left.reshape(rows, 128))
            rhs += [band_ref[0, 64:128], band_ref[1, 64:128]]
        if j == tiles - 1:
            lhs.append(right.reshape(rows, 128))
            rhs += [band_ref[0, 256:320], band_ref[1, 256:320]]
        c = jnp.dot(jnp.concatenate(lhs, axis=1), jnp.concatenate(rhs, axis=0), preferred_element_type=F32)
        cre.append(c[:, :128].astype(BF16))
        cim.append(c[:, 128:].astype(BF16))
    for s in range(subs):
        part = slice(s * pings, (s + 1) * pings)
        c = jnp.concatenate([jnp.concatenate([t[part] for t in cre], axis=1), jnp.concatenate([t[part] for t in cim], axis=1)], axis=0)
        wr = w_ref[0, s]
        wi = w_ref[1, s]
        out_ref[s, 0] = tdot(jnp.concatenate([wr, -wi], axis=0), c).astype(BF16)
        out_ref[s, 1] = tdot(jnp.concatenate([wi, wr], axis=0), c).astype(BF16)


def beams_of(samples, left, right, band, interp0):
    s, _, _, r = samples.shape
    b = interp0.shape[3]
    return pl.pallas_call(beams_kernel, out_shape=pltpu.VMEM((s, 2, b, r), BF16), name="beams", compiler_params=PARAMS)(
        samples, left, right, band, interp0
    )


def level_kernel(d, mix_ref, ph_own, ph_other, b_own, b_other, out_ref, turn_ref):
    fine = lax.axis_index("fine")
    k = fine & 1
    kids = ph_other.shape[0]
    n = out_ref.shape[1]
    base = pl.multiple_of((((fine >> 1) + d) & 3) * n, n)
    rows = pl.ds(base, n)
    for i, b in enumerate((b_own, b_other)):
        for s in range(kids):
            rhs = b[k * kids + s].reshape(-1, b.shape[3])
            for c in (0, 1):
                turn_ref[i * kids + s, c] = jnp.dot(mix_ref[i * kids + s, c, rows, :], rhs, preferred_element_type=F32)

    step = 16

    def body(j, carry):
        at = pl.ds(pl.multiple_of(j * step, step), step)
        there = pl.ds(pl.multiple_of(base + j * step, step), step)
        re = im = None
        for i, (ph, first) in enumerate(((ph_own, k * kids), (ph_other, 0))):
            for s in range(kids):
                c, t = cos_sin(ph[first + s, there, :].astype(F32))
                tr = turn_ref[i * kids + s, 0, at, :]
                ti = turn_ref[i * kids + s, 1, at, :]
                pr = c * tr - t * ti
                pi = t * tr + c * ti
                re = pr if re is None else re + pr
                im = pi if im is None else im + pi
        out_ref[0, at, :] = re.astype(out_ref.dtype)
        out_ref[1, at, :] = im.astype(out_ref.dtype)
        return carry

    lax.fori_loop(0, n // step, body, 0)


def level_part(d, dtype, *operands):
    mix, ph = operands[:2]
    s, _, n, _ = mix.shape
    n //= 4
    r = ph.shape[2]
    return pl.pallas_call(
        lambda *refs: level_kernel(d, *refs),
        in_specs=[WHOLE] * 5,
        out_specs=WHOLE,
        scratch_shapes=[pltpu.VMEM((s, 2, n, r), F32)],
        out_shape=pltpu.VMEM((2, n, r), dtype),
        name="level",
        compiler_params=PARAMS,
    )(*[near(x) for x in operands])


def turn_kernel(ph_ref, out_ref):
    step = 16

    def body(j, carry):
        at = pl.ds(pl.multiple_of(j * step, step), step)
        c, s = cos_sin(ph_ref[at, :].astype(F32))
        out_ref[0, at, :] = c
        out_ref[1, at, :] = s
        return carry

    lax.fori_loop(0, ph_ref.shape[0] // step, body, 0)


def turns(ph):
    return pl.pallas_call(
        turn_kernel,
        in_specs=[WHOLE],
        out_specs=WHOLE,
        out_shape=pltpu.VMEM((2,) + ph.shape, F32),
        name="turns",
        compiler_params=PARAMS,
    )(near(ph))


def mixed(us, vs, i):
    lhs = [x for u in us for x in ((u[0], -u[1]) if i == 0 else (u[1], u[0]))]
    rhs = [v[j] for v in vs for j in (0, 1)]
    return tdot(jnp.concatenate(lhs, axis=0), jnp.concatenate(rhs, axis=0))


def gather_kernel(*refs):
    half = len(refs) // 2
    for i in (0, 1):
        refs[-1][i] = mixed(refs[:half], refs[half:-1], i)


def gathered(us, vs):
    _, _, m = us[0].shape
    _, _, r = vs[0].shape
    return pl.pallas_call(
        gather_kernel,
        in_specs=[WHOLE] * (2 * len(us)),
        out_specs=WHOLE,
        out_shape=pltpu.VMEM((2, m, r), F32),
        name="gathered",
        compiler_params=PARAMS,
    )(*[near(x) for x in us], *[near(x) for x in vs])


def image_kernel(u_ref, low_ref, high_ref, part_ref, turn_ref, keep_ref, send_ref, acc_ref):
    own = core() == 0
    v = [jnp.concatenate([low_ref[j], high_ref[j]], axis=0) for j in (0, 1)]
    for i in (0, 1):
        acc_ref[i] = part_ref[i] + mixed((u_ref,), (v,), i)

    def body(c, carry):
        x = c & 3
        z = c >> 2
        halves = []
        for h in (0, 1):
            at = pl.ds(pl.multiple_of(c * 64 + h * 32, 32), 32)
            co = turn_ref[0, at, :]
            si = turn_ref[1, at, :]
            re = acc_ref[0, at, :]
            im = acc_ref[1, at, :]
            halves.append((co * re - si * im, si * re + co * im))
        for i in (0, 1):
            keep_ref[x, z, i] = jnp.where(own, halves[0][i], halves[1][i])
            send_ref[x, z, i] = jnp.where(own, halves[1][i], halves[0][i]).astype(BF16)
        return carry

    lax.fori_loop(0, 8, body, 0)


def image_parts(u, low, high, part, turn):
    _, m, r = turn.shape
    shape = (4, 2, 2, m // 16, r)
    return pl.pallas_call(
        image_kernel,
        in_specs=[WHOLE] * 5,
        out_specs=[WHOLE, WHOLE],
        scratch_shapes=[pltpu.VMEM((2, m, r), F32)],
        out_shape=[pltpu.VMEM(shape, F32), pltpu.VMEM(shape, BF16)],
        name="image",
        compiler_params=PARAMS,
    )(near(u), near(low), near(high), near(part), near(turn))


def join_kernel(*refs):
    total = refs[0][...]
    for ref in refs[1:-1]:
        total += ref[...].astype(F32)
    refs[-1][...] = total.astype(BF16)


def join(first, *rest):
    return pl.pallas_call(
        join_kernel,
        in_specs=[WHOLE] * (1 + len(rest)),
        out_specs=WHOLE,
        out_shape=pltpu.VMEM(first.shape, BF16),
        name="join",
        compiler_params=PARAMS,
    )(*[near(x) for x in (first,) + rest])


def finish_kernel(*refs):
    for i in (0, 1):
        total = refs[0][i]
        for ref in refs[1:-1]:
            total += ref[i].astype(F32)
        refs[-1][:, i, :] = total


def finish(first, *rest):
    i, m, r = first.shape
    return pl.pallas_call(
        finish_kernel,
        in_specs=[WHOLE] * (1 + len(rest)),
        out_specs=WHOLE,
        out_shape=jax.ShapeDtypeStruct((m, i, r), F32),
        name="finish",
        compiler_params=PARAMS,
    )(*[near(x) for x in (first,) + rest])


def program(echoes, exponents, replica, interp0, upsample1, phase1, upsample2, phase2):
    fine = lax.axis_index("fine")
    coarse = lax.axis_index("coarse")
    y = fine // 2
    k = fine % 2
    cx = coarse % 4
    cz = coarse // 4
    range_bins = echoes.shape[3]

    expo = jnp.transpose(exponents, (0, 2, 1))
    u2_other = swap_cores(upsample2)
    u1_other = swap_cores(upsample1)
    even, odd = ends(echoes, expo)
    even = lax.ppermute(even, "swath", [(0, 1), (1, 0), (2, 3), (3, 2)])
    odd = lax.ppermute(odd, "swath", [(0, 0), (1, 2), (2, 1), (3, 3)])
    ph_own = jnp.transpose(phase1, (1, 0, 2))
    ph_other = swap_cores(ph_own)
    band = bands(replica)
    (u2_far,) = pack((2,), upsample2, u2_other)
    u2_own, u2_after, u2_before = pack((0, 1, 3), upsample2, u2_other)
    u2_parts = [u2_own, u2_after, u2_far, u2_before]
    samples = prep(echoes, expo)
    u2_parts = [u2_parts[0]] + [shift_chips(u2_parts[d], d) for d in (1, 2, 3)]

    b_own = beams_of(samples, even, odd, band, interp0)
    b_other = swap_cores(b_own)

    mix, ph_other = weights(upsample1, u1_other, ph_other)
    operands = (mix, ph_own, ph_other, b_own, b_other)
    received = [shift_chips(level_part(d, BF16, *operands), d) for d in (2, 1, 3)]
    total = level_part(0, F32, *operands)
    for part in received:
        total += part.astype(F32)
    level = total.astype(BF16)
    before = shift_chips(level, 1)
    after = shift_chips(level, 3)
    half = level.shape[1] // 2
    low = shift_chips(before[:, :half], 1)
    high = shift_chips(after[:, half:], 3)

    ph2 = pick(pick(phase2.reshape(8, 4, 64, 2, range_bins), y, 1), k, 2).reshape(512, range_bins)
    turn = turns(ph2)

    keep, send = image_parts(
        u2_parts[2], low, high, gathered([u2_parts[0], u2_parts[1], u2_parts[3]], [level, before, after]), turn
    )
    other = swap_cores(send)
    narrow = (keep + other.astype(F32)).astype(BF16)

    def shares(z):
        first = pick(pick(keep, cx), z) + pick(pick(other, cx), z).astype(F32)
        return [first] + [shift_x(pick(pick(narrow, (cx + d) % 4), z), d) for d in (2, 1, 3)]

    far = swap_z(join(*shares(1 - cz)))
    return finish(*shares(cz), far)


def solution(mesh):
    in_specs = (
        P(("coarse", "fine"), None, None, "swath"),
        P(("coarse", "fine"), None, "swath"),
        P(),
        P(None, ("coarse", "fine"), None, None),
        P(None, ("coarse", "fine"), None, None),
        P(None, ("coarse", "fine"), "swath"),
        P("coarse", None, "fine", None),
        P(None, "coarse", "swath"),
    )
    out_specs = P(("coarse", "fine"), None, "swath")
    return jax.shard_map(program, mesh=mesh, in_specs=in_specs, out_specs=out_specs, check_vma=False)
```
